32 devices in a mesh: row: 4 (over y, x), col: 8 (over z, core).
Axes of the slice: x: 2, y: 2, z: 4, core: 2. Of those that a mesh axis runs over, the one named last changes fastest.
Arguments:
- amps_old: bfloat16 [1024, 262144], P(('row', 'col')), may hold values from -6 to 6
- other_terms: bfloat16 [1024, 262144], P(('row', 'col')), may hold values from -6 to 6
- occ_energy: float32 [32], replicated, may hold values from -1.5 to -0.5
- virt_energy: float32 [512], replicated, may hold values from 0.2 to 1.5
- integrals: bfloat16 [1024, 262144], P('row', 'col'), may hold values from -0.1875 to 0.1875
Outputs:
- amps_new: bfloat16 [1024, 262144], P(('row', 'col'))
The draws below stay inside these ranges and needn't reach their ends.
All inputs are finite; a program needn't handle non-finite values.
Results may differ from the reference program's by a relative error of at most 0.0055.
Values may be sent and summed in bfloat16 or wider, within the bound.
No kernel may reach another device: no remote copies, remote signals or barrier semaphores. Data moves between devices by JAX's collectives and lax.ppermute only.
A program may use at most 320 MiB of HBM per device.

```python
import jax
import jax.numpy as jnp
from jax import lax

O = 32
V = 512
CD_DEV = 256
IJ = 1024
VV = 262144
CD = 1024
N_ROW = 4


def steps_of(own_key, extent, pieces, least, high):
    gain = 1.0
    for dim, blocks in pieces:
        draws = jax.random.uniform(jax.random.fold_in(jax.random.fold_in(own_key, 6), dim), (blocks,), jnp.float32, least / len(pieces), high / len(pieces))
        gain = gain * jnp.repeat(jnp.exp(draws), extent[dim] // blocks).reshape((-1,) + (1,) * (len(extent) - 1 - dim))
    return gain


def centred(stream_key, dims, spread, limit, cuts=(), kind=jnp.bfloat16):
    loudness = steps_of(stream_key, dims, cuts, -0.22, 0.18) if cuts else 1.0
    drawn = jax.random.normal(stream_key, dims, jnp.float32) * spread * loudness
    return jnp.minimum(jnp.maximum(drawn, -limit), limit).astype(kind)


def setup_inputs(seed: int = 0) -> dict:
    streams_of = jax.random.split(jax.random.key(seed), 6)
    return {
        "amps_old": centred(streams_of[0], (IJ, VV), 1.0, 6.0, ((0, 32),)),
        "other_terms": centred(streams_of[1], (IJ, VV), 1.0, 6.0, ((0, 32),)),
        "occ_energy": jnp.clip(jax.random.uniform(streams_of[2], (O,), jnp.float32, -1.5, -0.5), -1.5, -0.5),
        "virt_energy": jnp.clip(jax.random.uniform(streams_of[3], (V,), jnp.float32, 0.2, 1.5), 0.2, 1.5),
        "integrals": centred(streams_of[4], (CD, VV), CD ** -0.5, 0.1875, ((0, 4), (1, 8))),
    }


def reference(amps_old, other_terms, occ_energy, virt_energy, integrals):
    pair_e = (occ_energy[:, None] + occ_energy[None, :]).reshape(O * O)
    virt_e = (virt_energy[:, None] + virt_energy[None, :]).reshape(V * V)
    cd_total = CD_DEV * N_ROW
    block_rows = 64
    blocks = (O * O) // block_rows

    def one_block(index):
        start = index * block_rows
        old_rows = lax.dynamic_slice_in_dim(amps_old, start, block_rows, 0)
        other_rows = lax.dynamic_slice_in_dim(other_terms, start, block_rows, 0)
        energy = lax.dynamic_slice_in_dim(pair_e, start, block_rows, 0)
        window = old_rows[:, :cd_total]
        ladder = jnp.zeros((block_rows, V * V), jnp.float32)
        for group in range(N_ROW):
            part = jnp.dot(window[:, group * CD_DEV:(group + 1) * CD_DEV],
                           integrals[group * CD_DEV:(group + 1) * CD_DEV, :],
                           preferred_element_type=jnp.float32).astype(jnp.bfloat16)
            ladder = ladder + part.astype(jnp.float32)
        denom = energy[:, None] - virt_e[None, :]
        increment = (ladder / denom).astype(jnp.bfloat16)
        updated = old_rows.astype(jnp.float32) + other_rows.astype(jnp.float32) / denom + increment.astype(jnp.float32)
        return updated.astype(jnp.bfloat16)

    result = lax.map(one_block, jnp.arange(blocks, dtype=jnp.int32))
    return result.reshape(O * O, V * V)
```

```python
import functools

import jax
import jax.numpy as jnp
from jax import lax
from jax.experimental import pallas as pl
from jax.experimental.pallas import tpu as pltpu
from jax.sharding import PartitionSpec as P

CHUNKS = 16


def pair_energy(pairs, occ_energy):
    count = occ_energy.shape[0]
    first = pairs // count
    second = pairs % count
    grid = jnp.arange(count, dtype=jnp.int32)
    e_first = jnp.sum(jnp.where(first[:, None] == grid[None, :], occ_energy[None, :], 0.0), axis=1)
    e_second = jnp.sum(
        jnp.where(second[:, None] == grid[None, :], occ_energy[None, :], 0.0), axis=1
    )
    return e_first + e_second


def contract_body(n_extra, t_ref, own_ref, far_ref, *refs):
    depth = own_ref.shape[0]
    outs = refs[n_extra:]
    acc = jnp.dot(t_ref[0, :, :depth], own_ref[...], preferred_element_type=jnp.float32)
    acc += jnp.dot(t_ref[0, :, depth:], far_ref[...], preferred_element_type=jnp.float32)
    for ref in refs[:n_extra]:
        acc += ref[...].astype(jnp.float32)
    rows = outs[0].shape[0]
    for m, out_ref in enumerate(outs):
        out_ref[...] = acc[m * rows : (m + 1) * rows].astype(out_ref.dtype)


def contract(panel, which, own, far, start, tile, extra=(), pieces=1):
    _, rows, depth2 = panel.shape
    depth, width = far.shape
    base = start // tile
    n_extra = len(extra)
    share = rows // pieces
    return pl.pallas_call(
        functools.partial(contract_body, n_extra),
        grid=(width // tile,),
        in_specs=[
            pl.BlockSpec((1, rows, depth2), lambda i: (which, 0, 0)),
            pl.BlockSpec((depth, tile), lambda i: (0, base + i)),
            pl.BlockSpec((depth, tile), lambda i: (0, i)),
        ]
        + [pl.BlockSpec((rows, tile), lambda i: (0, i))] * n_extra,
        out_specs=[pl.BlockSpec((share, tile), lambda i: (0, i))] * pieces,
        out_shape=[jax.ShapeDtypeStruct((share, width), jnp.bfloat16)] * pieces,
        cost_estimate=pl.CostEstimate(
            flops=2 * rows * depth2 * width,
            bytes_accessed=2 * width * (depth2 + rows * (1 + n_extra)),
            transcendentals=0,
        ),
    )(panel, own, far, *extra)


def update_body(start, cols, source_ref, va_ref, e_ref, vb_ref, old, other, *refs):
    out, old_buf, other_buf, moved_buf, new_buf, in_sem, out_sem = refs[-7:]
    n_col, rows, width = moved_buf.shape
    moved = refs[:n_col]
    virt = vb_ref.shape[1]

    def place(m):
        return pl.ds(pl.multiple_of(source_ref[m] * cols + start, 128), width)

    def fetches(m):
        return (
            pltpu.make_async_copy(old.at[:, place(m)], old_buf.at[m], in_sem.at[1, m]),
            pltpu.make_async_copy(other.at[:, place(m)], other_buf.at[m], in_sem.at[2, m]),
        )

    def store(m):
        return pltpu.make_async_copy(new_buf.at[m], out.at[:, place(m)], out_sem.at[m])

    for m in range(n_col):
        for copy in fetches(m):
            copy.start()
        pltpu.make_async_copy(moved[m], moved_buf.at[m], in_sem.at[0, m]).start()
    energy = jnp.broadcast_to(e_ref[...], (rows, virt))

    @pl.loop(0, n_col)
    def _(m):
        for copy in fetches(m):
            copy.wait()
        pltpu.make_async_copy(moved[0], moved_buf.at[m], in_sem.at[0, m]).wait()
        first = (source_ref[m] * cols + start) // virt
        for s in range(width // virt):
            part = pl.ds(s * virt, virt)
            inverse = 1.0 / (energy - (va_ref[first + s] + vb_ref[...]))
            top = other_buf[m, :, part].astype(jnp.float32) + moved_buf[m, :, part].astype(jnp.float32)
            new_buf[m, :, part] = (old_buf[m, :, part].astype(jnp.float32) + top * inverse).astype(new_buf.dtype)
        store(m).start()

    for m in range(n_col):
        store(m).wait()


def update(old, other, moved, source, energy, virt_energy, start, out):
    rows, total = old.shape
    n_col = len(moved)
    width = moved[0].shape[1]
    ins = [source, virt_energy, energy, virt_energy[None, :], old, other, *moved]
    specs = [
        pl.BlockSpec(memory_space=pltpu.SMEM),
        pl.BlockSpec(memory_space=pltpu.SMEM),
        pl.BlockSpec(memory_space=pltpu.VMEM),
        pl.BlockSpec(memory_space=pltpu.VMEM),
    ] + [pl.BlockSpec(memory_space=pl.ANY)] * (2 + n_col)
    alias = {}
    if out is not None:
        alias = {len(ins): 0}
        ins.append(out)
        specs.append(pl.BlockSpec(memory_space=pl.ANY))
    return pl.pallas_call(
        functools.partial(update_body, start, total // n_col),
        in_specs=specs,
        out_specs=pl.BlockSpec(memory_space=pl.ANY),
        out_shape=jax.ShapeDtypeStruct((rows, total), old.dtype),
        scratch_shapes=[pltpu.VMEM((n_col, rows, width), jnp.bfloat16)] * 4
        + [pltpu.SemaphoreType.DMA((3, n_col)), pltpu.SemaphoreType.DMA((n_col,))],
        input_output_aliases=alias,
        cost_estimate=pl.CostEstimate(
            flops=8 * n_col * rows * width, bytes_accessed=8 * n_col * rows * width, transcendentals=0
        ),
    )(*ins)


def local(amps_old, other_terms, occ_energy, virt_energy, integrals):
    n_row = lax.axis_size("row")
    n_col = lax.axis_size("col")
    row_id = lax.axis_index("row")
    col_id = lax.axis_index("col")
    per_dev = amps_old.shape[0]
    depth, cols = integrals.shape
    n_hi = n_row // 2
    hi, lo = row_id // 2, row_id % 2
    swap = [(r, r ^ 1) for r in range(n_row)]
    width = cols // CHUNKS

    def shift(value, d):
        perm = [(r, ((r // 2 + d) % n_hi) * 2 + r % 2) for r in range(n_row)]
        return lax.ppermute(value, "row", perm)

    far = []
    whole = integrals
    for k in range(CHUNKS):
        piece = whole[:, k * width : (k + 1) * width]
        whole, piece = lax.optimization_barrier((whole, piece))
        far.append(lax.ppermute(piece, "row", swap))

    window = amps_old[:, : depth * n_row]

    def pick(g):
        return lax.dynamic_slice_in_dim(window, g * 2 * depth, 2 * depth, 1)

    mine = [pick(hi)] + [shift(pick((hi - d) % n_hi), -d) for d in range(1, n_hi)]
    panel = lax.all_gather(jnp.stack(mine), "col", axis=1, tiled=True)
    flipped = jnp.concatenate([panel[..., depth:], panel[..., :depth]], axis=-1)
    panel = jnp.where(lo == 0, panel, flipped)
    source = col_id ^ jnp.arange(n_col, dtype=jnp.int32)
    blocks = panel.reshape(n_hi, n_col, per_dev, 2 * depth)
    panel = jnp.concatenate(
        [lax.dynamic_slice_in_dim(blocks, source[m], 1, 1) for m in range(n_col)], axis=1
    ).reshape(panel.shape)

    first_pair = (row_id * n_col + col_id) * per_dev
    energy = pair_energy(first_pair + jnp.arange(per_dev, dtype=jnp.int32), occ_energy)[:, None]

    out = None
    for k in range(CHUNKS):
        start = k * width
        tile = min(1024, width)
        parts = [contract(panel, d, integrals, far[k], start, tile)[0] for d in range(1, n_hi)]
        got = [shift(part, d) for d, part in enumerate(parts, 1)]
        ladder = contract(panel, 0, integrals, far[k], start, tile, got, n_col)
        moved = [ladder[0]]
        for m in range(1, n_col):
            moved.append(lax.ppermute(ladder[m], "col", [(c, c ^ m) for c in range(n_col)]))
        out = update(amps_old, other_terms, moved, source, energy, virt_energy, start, out)
    return out


def solution(mesh):
    return jax.shard_map(
        local,
        mesh=mesh,
        in_specs=(P(("row", "col"), None), P(("row", "col"), None), P(), P(), P("row", "col")),
        out_specs=P(("row", "col"), None),
        check_vma=False,
    )
```

```python
import functools

import jax
import jax.numpy as jnp
from jax import lax
from jax.experimental import pallas as pl
from jax.experimental.pallas import tpu as pltpu
from jax.sharding import PartitionSpec as P

UNITS = 3
TILES = 2
AHEAD = 2
LAG = 4
VMEM = 67_000_000


def pair_energy(pairs, occ_energy):
    count = occ_energy.shape[0]
    first = pairs // count
    second = pairs % count
    grid = jnp.arange(count, dtype=jnp.int32)
    e_first = jnp.sum(jnp.where(first[:, None] == grid[None, :], occ_energy[None, :], 0.0), axis=1)
    e_second = jnp.sum(
        jnp.where(second[:, None] == grid[None, :], occ_energy[None, :], 0.0), axis=1
    )
    return e_first + e_second


def chunks_of(cols, virt):
    step = UNITS * virt
    return [(start, min(step, cols - start)) for start in range(0, cols, step)]


class Contract:
    def __init__(self, panel, which, own, far, start, extra=(), blocks=False, ahead=None):
        self.which, self.start, self.blocks, self.ahead = which, start, blocks, ahead
        self.n_extra = len(extra)
        self.n_col, _, self.per_dev, self.depth2 = panel.shape
        self.depth, self.width = far.shape
        self.rows = self.n_col * self.per_dev
        tiles = TILES + blocks
        self.tiles = tiles if self.width % (tiles * 128) == 0 else TILES if self.width % (TILES * 128) == 0 else 1
        self.tile = self.width // self.tiles
        self.ins = [panel, own, far, *extra]
        self.in_specs = [pl.BlockSpec(memory_space=pl.ANY)] * len(self.ins)
        bf16 = jnp.bfloat16
        pieces, share = (self.n_col // 2, 2 * self.per_dev) if blocks else (len(which), self.rows)
        self.pieces = pieces
        self.out_shape = [jax.ShapeDtypeStruct((share, self.width), bf16)] * pieces
        self.scratch = [
            pltpu.VMEM((len(which), self.n_col, self.per_dev, self.depth2), bf16),
            pltpu.VMEM((2, self.depth, self.width), bf16),
            pltpu.VMEM((max(self.n_extra, 1), self.rows, self.width), bf16),
            pltpu.VMEM((pieces, share, self.width), bf16),
            pltpu.SemaphoreType.DMA((len(which),)),
            pltpu.SemaphoreType.DMA((2 + self.n_extra, self.tiles)),
            pltpu.SemaphoreType.DMA((pieces, self.tiles)),
        ]
        if ahead:
            self.out_shape.append(jax.ShapeDtypeStruct((self.depth, ahead[1]), bf16))
            self.scratch += [pltpu.VMEM((self.depth, ahead[1]), bf16), pltpu.SemaphoreType.DMA((2,))]
        self.flops = 2 * self.rows * self.depth2 * self.width * len(which)
        self.bytes = 2 * self.width * (self.depth2 + self.rows * (len(which) + self.n_extra))

    def bind(self, ins, outs, scratch):
        (self.panel, self.own, self.far), self.extra = ins[:3], ins[3:]
        self.outs = outs[: self.pieces]
        self.t_buf, self.in_buf, self.extra_buf, self.out_buf = scratch[:4]
        self.t_sem, self.in_sem, self.out_sem = scratch[4:7]
        if self.ahead:
            self.later, (self.ahead_buf, self.ahead_sem) = outs[self.pieces], scratch[7:]

    def loads(self, i):
        at = pl.multiple_of(i * self.tile, 128)
        here = pl.ds(at, self.tile)
        there = pl.ds(pl.multiple_of(self.start + at, 128), self.tile)
        pairs = [(self.own.at[:, there], self.in_buf.at[0, :, here]), (self.far.at[:, here], self.in_buf.at[1, :, here])]
        pairs += [(ref.at[:, here], self.extra_buf.at[e, :, here]) for e, ref in enumerate(self.extra)]
        return [pltpu.make_async_copy(a, b, self.in_sem.at[e, i]) for e, (a, b) in enumerate(pairs)]

    def stores(self, i):
        here = pl.ds(pl.multiple_of(i * self.tile, 128), self.tile)
        return [
            pltpu.make_async_copy(self.out_buf.at[m, :, here], ref.at[:, here], self.out_sem.at[m, i])
            for m, ref in enumerate(self.outs)
        ]

    def panels(self):
        return [
            pltpu.make_async_copy(self.panel.at[:, d], self.t_buf.at[q], self.t_sem.at[q])
            for q, d in enumerate(self.which)
        ]

    def ahead_load(self):
        start, width = self.ahead
        return pltpu.make_async_copy(self.own.at[:, pl.ds(start, width)], self.ahead_buf, self.ahead_sem.at[0])

    def ahead_store(self):
        return pltpu.make_async_copy(self.ahead_buf, self.later, self.ahead_sem.at[1])

    def begin(self):
        for copy in self.panels():
            copy.start()
        for i in range(self.tiles):
            for copy in self.loads(i):
                copy.start()
        if self.ahead:
            self.ahead_load().start()

    def run(self):
        for copy in self.panels():
            copy.wait()
        ts = [
            jnp.concatenate([self.t_buf[q, m] for m in range(self.n_col)], axis=0)
            for q in range(len(self.which))
        ]

        @pl.loop(0, self.tiles)
        def _(i):
            for copy in self.loads(i):
                copy.wait()
            here = pl.ds(pl.multiple_of(i * self.tile, 128), self.tile)
            for q, t in enumerate(ts):
                acc = jnp.dot(t[:, : self.depth], self.in_buf[0, :, here], preferred_element_type=jnp.float32)
                acc += jnp.dot(t[:, self.depth :], self.in_buf[1, :, here], preferred_element_type=jnp.float32)
                for e in range(self.n_extra):
                    acc += self.extra_buf[e, :, here].astype(jnp.float32)
                if self.blocks:
                    share = 2 * self.per_dev
                    for m in range(self.pieces):
                        rows = acc[m * share : (m + 1) * share]
                        self.out_buf[m, :, here] = rows.astype(self.out_buf.dtype)
                else:
                    self.out_buf[q, :, here] = acc.astype(self.out_buf.dtype)
            for copy in self.stores(i):
                copy.start()

        if self.ahead:
            self.ahead_load().wait()
            self.ahead_store().start()

    def end(self):
        for i in range(self.tiles):
            for copy in self.stores(i):
                copy.wait()
        if self.ahead:
            self.ahead_store().wait()


class Update:
    def __init__(self, old, other, moved, source, energy, virt_energy, start, out):
        self.start, self.prev, self.host = start, out, None
        if isinstance(out, Update):
            self.prev, self.host = None, out
        rows, columns = old.shape
        self.n_col, self.width = len(moved), moved[0].shape[1]
        self.cols, self.rows, self.virt = columns // self.n_col, rows, virt_energy.shape[0]
        self.ins = [source, virt_energy, energy, virt_energy[None, :], old, other, *moved]
        self.in_specs = [
            pl.BlockSpec(memory_space=pltpu.SMEM),
            pl.BlockSpec(memory_space=pltpu.SMEM),
            pl.BlockSpec(memory_space=pltpu.VMEM),
            pl.BlockSpec(memory_space=pltpu.VMEM),
        ] + [pl.BlockSpec(memory_space=pl.ANY)] * (2 + self.n_col)
        if self.prev is not None:
            self.ins.append(out)
            self.in_specs.append(pl.BlockSpec(memory_space=pl.ANY))
        self.out_shape = [] if self.host else [jax.ShapeDtypeStruct((rows, columns), old.dtype)]
        self.scratch = [pltpu.VMEM((self.n_col, rows, self.width), jnp.bfloat16)] * 4 + [
            pltpu.SemaphoreType.DMA((3, self.n_col)),
            pltpu.SemaphoreType.DMA((self.n_col,)),
        ]
        self.flops = 8 * self.n_col * rows * self.width
        self.bytes = 8 * self.n_col * rows * self.width

    def bind(self, ins, outs, scratch):
        self.source, self.va, self.e, self.vb, self.old, self.other = ins[:6]
        self.moved = ins[6 : 6 + self.n_col]
        self.out = self.host.out if self.host else outs[0]
        self.old_buf, self.other_buf, self.moved_buf, self.new_buf, self.in_sem, self.out_sem = scratch

    def place(self, m):
        return pl.ds(pl.multiple_of(self.source[m] * self.cols + self.start, 128), self.width)

    def loads(self, m):
        return [
            pltpu.make_async_copy(self.old.at[:, self.place(m)], self.old_buf.at[m], self.in_sem.at[0, m]),
            pltpu.make_async_copy(self.other.at[:, self.place(m)], self.other_buf.at[m], self.in_sem.at[1, m]),
        ]

    def arrive(self, m, which):
        rows = pl.ds(which % 2 * self.rows, self.rows)
        return pltpu.make_async_copy(self.moved[which].at[rows], self.moved_buf.at[m], self.in_sem.at[2, m])

    def store(self, m):
        return pltpu.make_async_copy(self.new_buf.at[m], self.out.at[:, self.place(m)], self.out_sem.at[m])

    def begin(self):
        for m in range(self.n_col):
            self.arrive(m, m).start()

        @pl.loop(0, self.n_col)
        def _(m):
            for copy in self.loads(m):
                copy.start()

    def run(self):
        virt = self.virt
        energy = jnp.broadcast_to(self.e[...], (self.rows, virt))

        @pl.loop(0, self.n_col)
        def _(m):
            for copy in [*self.loads(m), self.arrive(m, 0)]:
                copy.wait()
            first = (self.source[m] * self.cols + self.start) // virt

            @pl.loop(0, self.width // virt)
            def _(s):
                part = pl.ds(pl.multiple_of(s * virt, 128), virt)
                inverse = 1.0 / (energy - (self.va[first + s] + self.vb[...]))
                top = self.other_buf[m, :, part].astype(jnp.float32) + self.moved_buf[m, :, part].astype(jnp.float32)
                new = self.old_buf[m, :, part].astype(jnp.float32) + top * inverse
                self.new_buf[m, :, part] = new.astype(self.new_buf.dtype)

            self.store(m).start()

    def end(self):
        @pl.loop(0, self.n_col)
        def _(m):
            self.store(m).wait()


def kernel(jobs, *refs):
    refs = list(refs)
    take = lambda n: [refs.pop(0) for _ in range(n)]
    ins = [take(len(job.ins)) for job in jobs]
    outs = [take(len(job.out_shape)) for job in jobs]
    for job, job_ins, job_outs in zip(jobs, ins, outs):
        job.bind(job_ins, job_outs, take(len(job.scratch)))
    for job in jobs:
        job.begin()
    for job in jobs:
        job.run()
    for job in jobs:
        job.end()


def call(*jobs):
    jobs = [job for job in jobs if job is not None]
    alias, n_in, n_out = {}, 0, 0
    for job in jobs:
        n_in += len(job.ins)
        if getattr(job, "prev", None) is not None:
            alias[n_in - 1] = n_out
        n_out += len(job.out_shape)
    flat = lambda name: [x for job in jobs for x in getattr(job, name)]
    results = pl.pallas_call(
        functools.partial(kernel, jobs),
        in_specs=flat("in_specs"),
        out_specs=[pl.BlockSpec(memory_space=pl.ANY)] * n_out,
        out_shape=flat("out_shape"),
        scratch_shapes=flat("scratch"),
        input_output_aliases=alias,
        compiler_params=pltpu.CompilerParams(vmem_limit_bytes=VMEM),
        cost_estimate=pl.CostEstimate(
            flops=sum(job.flops for job in jobs),
            bytes_accessed=sum(job.bytes for job in jobs),
            transcendentals=0,
        ),
    )(*flat("ins"))
    results = list(results)
    return [[results.pop(0) for _ in job.out_shape] for job in jobs]


def local(amps_old, other_terms, occ_energy, virt_energy, integrals):
    n_row = lax.axis_size("row")
    n_col = lax.axis_size("col")
    row_id = lax.axis_index("row")
    col_id = lax.axis_index("col")
    per_dev = amps_old.shape[0]
    depth, cols = integrals.shape
    n_hi = n_row // 2
    hi, lo = row_id // 2, row_id % 2
    chunks = chunks_of(cols, virt_energy.shape[0])
    count = len(chunks)
    swap = [(r, r ^ 1) for r in range(n_row)]

    def shift(value, d):
        perm = [(r, ((r // 2 + d) % n_hi) * 2 + r % 2) for r in range(n_row)]
        return lax.ppermute(value, "row", perm)

    def trade(value, m):
        return lax.ppermute(value, "col", [(c, c ^ m) for c in range(n_col)])

    far = {}

    def fetch(k, piece):
        far[k] = lax.ppermute(piece, "row", swap)

    whole = integrals
    for k, (start, width) in enumerate(chunks[:AHEAD]):
        piece = whole[:, start : start + width]
        whole, piece = lax.optimization_barrier((whole, piece))
        fetch(k, piece)

    def pick(g):
        groups = [g * 2 + lo, g * 2 + 1 - lo]
        window = amps_old[:, : depth * n_row]
        return jnp.concatenate([lax.dynamic_slice_in_dim(window, q * depth, depth, 1) for q in groups], axis=1)

    mine = [pick(hi)]
    for d in range(1, n_hi):
        mine.append(shift(pick((hi - d) % n_hi), -d))
    panel = jnp.stack(mine)[None]
    step = n_col // 2
    while step:
        panel = jnp.stack([panel, trade(panel, step)], axis=1).reshape(-1, *panel.shape[1:])
        step //= 2
    source = col_id ^ jnp.arange(n_col, dtype=jnp.int32)

    first_pair = (row_id * n_col + col_id) * per_dev
    energy = pair_energy(first_pair + jnp.arange(per_dev, dtype=jnp.int32), occ_energy)[:, None]

    moved = {}
    out = None

    def renew(k, onto):
        start = chunks[k][0]
        return Update(amps_old, other_terms, moved[k], source, energy, virt_energy, start, onto)

    for k, (start, width) in enumerate(chunks):
        ahead = chunks[k + AHEAD] if k + AHEAD < count else None
        job = Contract(panel, range(1, n_hi), integrals, far[k], start, ahead=ahead)
        if k >= LAG:
            parts, (out,) = call(job, renew(k - LAG, out))
        else:
            (parts,) = call(job)
        if ahead:
            fetch(k + AHEAD, parts.pop())
        got = [shift(part, d) for d, part in enumerate(parts, 1)]
        (ladder,) = call(Contract(panel, (0,), integrals, far[k], start, got, blocks=True))
        moved[k] = []
        for m, block in enumerate(ladder):
            if m:
                block = trade(block, 2 * m)
            moved[k] += [block, trade(block, 1)]
    for k in (count - 4, count - 3):
        ((out,),) = call(renew(k, out))
    first = renew(count - 2, out)
    (out,), _ = call(first, renew(count - 1, first))
    return out


def solution(mesh):
    return jax.shard_map(
        local,
        mesh=mesh,
        in_specs=(P(("row", "col"), None), P(("row", "col"), None), P(), P(), P("row", "col")),
        out_specs=P(("row", "col"), None),
        check_vma=False,
    )
```

```python
import functools

import jax
import jax.numpy as jnp
from jax import lax
from jax.experimental import pallas as pl
from jax.experimental.pallas import tpu as pltpu
from jax.sharding import PartitionSpec as P

UNITS = 3
TILES = 2
AHEAD = 3
LAG = 4
VMEM = 67_000_000


def pair_energy(pairs, occ_energy):
    count = occ_energy.shape[0]
    first = pairs // count
    second = pairs % count
    grid = jnp.arange(count, dtype=jnp.int32)
    e_first = jnp.sum(jnp.where(first[:, None] == grid[None, :], occ_energy[None, :], 0.0), axis=1)
    e_second = jnp.sum(
        jnp.where(second[:, None] == grid[None, :], occ_energy[None, :], 0.0), axis=1
    )
    return e_first + e_second


def chunks_of(cols, virt):
    step = UNITS * virt
    edges = [0, *range(cols % step or step, cols + 1, step)]
    return [(a, b - a) for a, b in zip(edges, edges[1:])]


class Contract:
    def __init__(self, panel, which, own, far, start, extra=(), blocks=False, ahead=None):
        self.which, self.start, self.blocks, self.ahead = which, start, blocks, ahead
        self.n_extra = len(extra)
        self.n_col, _, self.per_dev, self.depth2 = panel.shape
        self.depth, self.width = far.shape
        self.rows = self.n_col * self.per_dev
        tiles = TILES + blocks
        self.tiles = tiles if self.width % (tiles * 128) == 0 else TILES if self.width % (TILES * 128) == 0 else 1
        self.tile = self.width // self.tiles
        self.ins = [panel, own, far, *extra]
        self.in_specs = [pl.BlockSpec(memory_space=pl.ANY)] * len(self.ins)
        bf16 = jnp.bfloat16
        pieces, share = (self.n_col // 2, 2 * self.per_dev) if blocks else (len(which), self.rows)
        self.pieces = pieces
        self.out_shape = [jax.ShapeDtypeStruct((share, self.width), bf16)] * pieces
        self.scratch = [
            pltpu.VMEM((len(which), self.n_col, self.per_dev, self.depth2), bf16),
            pltpu.VMEM((2, self.depth, self.width), bf16),
            pltpu.VMEM((max(self.n_extra, 1), self.rows, self.width), bf16),
            pltpu.VMEM((pieces, share, self.width), bf16),
            pltpu.SemaphoreType.DMA((len(which),)),
            pltpu.SemaphoreType.DMA((2 + self.n_extra, self.tiles)),
            pltpu.SemaphoreType.DMA((pieces, self.tiles)),
        ]
        if ahead:
            self.out_shape.append(jax.ShapeDtypeStruct((self.depth, ahead[1]), bf16))
            self.scratch += [pltpu.VMEM((self.depth, ahead[1]), bf16), pltpu.SemaphoreType.DMA((2,))]
        self.flops = 2 * self.rows * self.depth2 * self.width * len(which)
        self.bytes = 2 * self.width * (self.depth2 + self.rows * (len(which) + self.n_extra))

    def bind(self, ins, outs, scratch):
        (self.panel, self.own, self.far), self.extra = ins[:3], ins[3:]
        self.outs = outs[: self.pieces]
        self.t_buf, self.in_buf, self.extra_buf, self.out_buf = scratch[:4]
        self.t_sem, self.in_sem, self.out_sem = scratch[4:7]
        if self.ahead:
            self.later, (self.ahead_buf, self.ahead_sem) = outs[self.pieces], scratch[7:]

    def loads(self, i):
        at = pl.multiple_of(i * self.tile, 128)
        here = pl.ds(at, self.tile)
        there = pl.ds(pl.multiple_of(self.start + at, 128), self.tile)
        pairs = [(self.own.at[:, there], self.in_buf.at[0, :, here]), (self.far.at[:, here], self.in_buf.at[1, :, here])]
        pairs += [(ref.at[:, here], self.extra_buf.at[e, :, here]) for e, ref in enumerate(self.extra)]
        return [pltpu.make_async_copy(a, b, self.in_sem.at[e, i]) for e, (a, b) in enumerate(pairs)]

    def stores(self, i):
        here = pl.ds(pl.multiple_of(i * self.tile, 128), self.tile)
        return [
            pltpu.make_async_copy(self.out_buf.at[m, :, here], ref.at[:, here], self.out_sem.at[m, i])
            for m, ref in enumerate(self.outs)
        ]

    def panels(self):
        return [
            pltpu.make_async_copy(self.panel.at[:, d], self.t_buf.at[q], self.t_sem.at[q])
            for q, d in enumerate(self.which)
        ]

    def ahead_load(self):
        start, width = self.ahead
        return pltpu.make_async_copy(self.own.at[:, pl.ds(start, width)], self.ahead_buf, self.ahead_sem.at[0])

    def ahead_store(self):
        return pltpu.make_async_copy(self.ahead_buf, self.later, self.ahead_sem.at[1])

    def begin(self):
        for copy in self.panels():
            copy.start()
        for i in range(self.tiles):
            for copy in self.loads(i):
                copy.start()
        if self.ahead:
            self.ahead_load().start()

    def run(self):
        for copy in self.panels():
            copy.wait()
        ts = [
            jnp.concatenate([self.t_buf[q, m] for m in range(self.n_col)], axis=0)
            for q in range(len(self.which))
        ]

        @pl.loop(0, self.tiles)
        def _(i):
            for copy in self.loads(i):
                copy.wait()
            here = pl.ds(pl.multiple_of(i * self.tile, 128), self.tile)
            for q, t in enumerate(ts):
                acc = jnp.dot(t[:, : self.depth], self.in_buf[0, :, here], preferred_element_type=jnp.float32)
                acc += jnp.dot(t[:, self.depth :], self.in_buf[1, :, here], preferred_element_type=jnp.float32)
                for e in range(self.n_extra):
                    acc += self.extra_buf[e, :, here].astype(jnp.float32)
                if self.blocks:
                    share = 2 * self.per_dev
                    for m in range(self.pieces):
                        rows = acc[m * share : (m + 1) * share]
                        self.out_buf[m, :, here] = rows.astype(self.out_buf.dtype)
                else:
                    self.out_buf[q, :, here] = acc.astype(self.out_buf.dtype)
            for copy in self.stores(i):
                copy.start()

        if self.ahead:
            self.ahead_load().wait()
            self.ahead_store().start()

    def end(self):
        for i in range(self.tiles):
            for copy in self.stores(i):
                copy.wait()
        if self.ahead:
            self.ahead_store().wait()


class Update:
    def __init__(self, old, other, moved, source, energy, virt_energy, start, out):
        self.start, self.prev = start, out
        rows, columns = old.shape
        self.n_col, self.width = len(moved), moved[0].shape[1]
        self.cols, self.rows, self.virt = columns // self.n_col, rows, virt_energy.shape[0]
        self.ins = [source, virt_energy, energy, virt_energy[None, :], old, other, *moved]
        self.in_specs = [
            pl.BlockSpec(memory_space=pltpu.SMEM),
            pl.BlockSpec(memory_space=pltpu.SMEM),
            pl.BlockSpec(memory_space=pltpu.VMEM),
            pl.BlockSpec(memory_space=pltpu.VMEM),
        ] + [pl.BlockSpec(memory_space=pl.ANY)] * (2 + self.n_col)
        if self.prev is not None:
            self.ins.append(out)
            self.in_specs.append(pl.BlockSpec(memory_space=pl.ANY))
        self.out_shape = [jax.ShapeDtypeStruct((rows, columns), old.dtype)]
        self.scratch = [pltpu.VMEM((self.n_col, rows, self.width), jnp.bfloat16)] * 4 + [
            pltpu.SemaphoreType.DMA((3, self.n_col)),
            pltpu.SemaphoreType.DMA((self.n_col,)),
        ]
        self.flops = 8 * self.n_col * rows * self.width
        self.bytes = 8 * self.n_col * rows * self.width

    def bind(self, ins, outs, scratch):
        self.source, self.va, self.e, self.vb, self.old, self.other = ins[:6]
        self.moved = ins[6 : 6 + self.n_col]
        (self.out,) = outs
        self.old_buf, self.other_buf, self.moved_buf, self.new_buf, self.in_sem, self.out_sem = scratch

    def place(self, m):
        return pl.ds(pl.multiple_of(self.source[m] * self.cols + self.start, 128), self.width)

    def loads(self, m):
        return [
            pltpu.make_async_copy(self.old.at[:, self.place(m)], self.old_buf.at[m], self.in_sem.at[0, m]),
            pltpu.make_async_copy(self.other.at[:, self.place(m)], self.other_buf.at[m], self.in_sem.at[1, m]),
        ]

    def arrive(self, m, which):
        rows = pl.ds(which % 2 * self.rows, self.rows)
        return pltpu.make_async_copy(self.moved[which].at[rows], self.moved_buf.at[m], self.in_sem.at[2, m])

    def store(self, m):
        return pltpu.make_async_copy(self.new_buf.at[m], self.out.at[:, self.place(m)], self.out_sem.at[m])

    def begin(self):
        for m in range(self.n_col):
            self.arrive(m, m).start()

        @pl.loop(0, self.n_col)
        def _(m):
            for copy in self.loads(m):
                copy.start()

    def run(self):
        virt = self.virt
        energy = jnp.broadcast_to(self.e[...], (self.rows, virt))

        @pl.loop(0, self.n_col)
        def _(m):
            for copy in [*self.loads(m), self.arrive(m, 0)]:
                copy.wait()
            first = (self.source[m] * self.cols + self.start) // virt

            @pl.loop(0, self.width // virt)
            def _(s):
                part = pl.ds(pl.multiple_of(s * virt, 128), virt)
                inverse = 1.0 / (energy - (self.va[first + s] + self.vb[...]))
                top = self.other_buf[m, :, part].astype(jnp.float32) + self.moved_buf[m, :, part].astype(jnp.float32)
                new = self.old_buf[m, :, part].astype(jnp.float32) + top * inverse
                self.new_buf[m, :, part] = new.astype(self.new_buf.dtype)

            self.store(m).start()

    def end(self):
        @pl.loop(0, self.n_col)
        def _(m):
            self.store(m).wait()


def kernel(jobs, *refs):
    refs = list(refs)
    take = lambda n: [refs.pop(0) for _ in range(n)]
    ins = [take(len(job.ins)) for job in jobs]
    outs = [take(len(job.out_shape)) for job in jobs]
    for job, job_ins, job_outs in zip(jobs, ins, outs):
        job.bind(job_ins, job_outs, take(len(job.scratch)))
    for job in jobs:
        job.begin()
    for job in jobs:
        job.run()
    for job in jobs:
        job.end()


def call(*jobs):
    jobs = [job for job in jobs if job is not None]
    alias, n_in, n_out = {}, 0, 0
    for job in jobs:
        n_in += len(job.ins)
        if getattr(job, "prev", None) is not None:
            alias[n_in - 1] = n_out
        n_out += len(job.out_shape)
    flat = lambda name: [x for job in jobs for x in getattr(job, name)]
    results = pl.pallas_call(
        functools.partial(kernel, jobs),
        in_specs=flat("in_specs"),
        out_specs=[pl.BlockSpec(memory_space=pl.ANY)] * n_out,
        out_shape=flat("out_shape"),
        scratch_shapes=flat("scratch"),
        input_output_aliases=alias,
        compiler_params=pltpu.CompilerParams(vmem_limit_bytes=VMEM),
        cost_estimate=pl.CostEstimate(
            flops=sum(job.flops for job in jobs),
            bytes_accessed=sum(job.bytes for job in jobs),
            transcendentals=0,
        ),
    )(*flat("ins"))
    results = list(results)
    return [[results.pop(0) for _ in job.out_shape] for job in jobs]


def local(amps_old, other_terms, occ_energy, virt_energy, integrals):
    n_row = lax.axis_size("row")
    n_col = lax.axis_size("col")
    row_id = lax.axis_index("row")
    col_id = lax.axis_index("col")
    per_dev = amps_old.shape[0]
    depth, cols = integrals.shape
    n_hi = n_row // 2
    hi, lo = row_id // 2, row_id % 2
    chunks = chunks_of(cols, virt_energy.shape[0])
    count = len(chunks)
    swap = [(r, r ^ 1) for r in range(n_row)]

    def shift(value, d):
        perm = [(r, ((r // 2 + d) % n_hi) * 2 + r % 2) for r in range(n_row)]
        return lax.ppermute(value, "row", perm)

    def trade(value, m):
        return lax.ppermute(value, "col", [(c, c ^ m) for c in range(n_col)])

    far = {}

    def fetch(k, piece):
        far[k] = lax.ppermute(piece, "row", swap)

    whole = integrals
    for k, (start, width) in enumerate(chunks[:AHEAD]):
        piece = whole[:, start : start + width]
        whole, piece = lax.optimization_barrier((whole, piece))
        fetch(k, piece)

    def pick(g):
        groups = [g * 2 + lo, g * 2 + 1 - lo]
        window = amps_old[:, : depth * n_row]
        return jnp.concatenate([lax.dynamic_slice_in_dim(window, q * depth, depth, 1) for q in groups], axis=1)

    mine = [pick(hi)]
    for d in range(1, n_hi):
        mine.append(shift(pick((hi - d) % n_hi), -d))
    panel = jnp.stack(mine)[None]
    step = n_col // 2
    while step:
        panel = jnp.stack([panel, trade(panel, step)], axis=1).reshape(-1, *panel.shape[1:])
        step //= 2
    source = col_id ^ jnp.arange(n_col, dtype=jnp.int32)

    first_pair = (row_id * n_col + col_id) * per_dev
    energy = pair_energy(first_pair + jnp.arange(per_dev, dtype=jnp.int32), occ_energy)[:, None]

    moved = {}
    out = None

    def renew(k, onto):
        start = chunks[k][0]
        return Update(amps_old, other_terms, moved[k], source, energy, virt_energy, start, onto)

    far[1], energy, source = lax.optimization_barrier((far[1], energy, source))
    for k, (start, width) in enumerate(chunks):
        ahead = chunks[k + AHEAD] if k + AHEAD < count else None
        job = Contract(panel, range(1, n_hi), integrals, far[k], start, ahead=ahead)
        if k >= LAG:
            parts, (out,) = call(job, renew(k - LAG, out))
        else:
            (parts,) = call(job)
        if ahead:
            fetch(k + AHEAD, parts.pop())
        got = [shift(part, d) for d, part in enumerate(parts, 1)]
        (ladder,) = call(Contract(panel, (0,), integrals, far[k], start, got, blocks=True))
        moved[k] = []
        for m, block in enumerate(ladder):
            if m:
                block = trade(block, 2 * m)
            moved[k] += [block, trade(block, 1)]
    for k in range(count - LAG, count):
        ((out,),) = call(renew(k, out))
    return out


def solution(mesh):
    return jax.shard_map(
        local,
        mesh=mesh,
        in_specs=(P(("row", "col"), None), P(("row", "col"), None), P(), P(), P("row", "col")),
        out_specs=P(("row", "col"), None),
        check_vma=False,
    )
```
